32 devices in a mesh: grp: 2 (over x), filt: 8 (over z, y), sky: 2 (over core).
Axes of the slice: x: 2, y: 2, z: 4, core: 2. Of those that a mesh axis runs over, the one named last changes fastest.
Arguments:
- strain: bfloat16 [2, 6, 524288], P(None, 'grp', 'filt'), parts along dimension 1, may hold values from -4 to 4
- templates: bfloat16 [2, 4, 524288], P(None, 'sky', 'filt'), may hold values from -6 to 6
- lengths: int32 [4], P('sky'), may hold values from 131072 to 524288
- antenna: bfloat16 [2, 3, 3072], P(None, None, 'sky'), may hold values from -1 to 1
- delays: int32 [3, 3072], P(None, 'sky'), may hold values from -48 to 48
Outputs:
- peak: float32 [2, 2048, 3072], P('grp', 'filt', 'sky'), parts along dimension 0
The draws below stay inside these ranges and needn't reach their ends.
There are 2 independent parts, one for each index of `grp`. The reference program is written for one: setup_inputs(seed, part) draws one part's arguments, and reference() takes and returns one part's arrays. A program takes and returns all parts, laid end to end along the dimension named above; an argument that names none is the same for every part. Nothing has to cross between parts.
All inputs are finite; a program needn't handle non-finite values.
Results may differ from the reference program's by a relative error of at most 0.018.
Values may be sent and summed in bfloat16 or wider, within the bound.
A program may use at most 64 MiB of HBM per device.

```python
import math
import jax
import jax.numpy as jnp
from jax import lax

N1 = 2048
N2 = 512
NF = 1048576
NH = 524288
DET = 3
SKY = 3072
DM = 48
KT = 4
K2 = 3
KO = 1


def plant(entries, rng, low, high):
    longest = entries.shape.index(max(entries.shape))
    spots = []
    for shift in (0, 1):
        where = [jax.random.randint(jax.random.fold_in(rng, axis), (), 0, length) for axis, length in enumerate(entries.shape)]
        where[longest] = (where[longest] + shift) % entries.shape[longest]
        spots.append(tuple(where))
    return entries.at[spots[0]].set(low).at[spots[1]].set(high)


def steps_of(own_key, extent, pieces, low, top_value):
    def one(position, parts):
        draws = jax.random.uniform(jax.random.fold_in(jax.random.fold_in(own_key, 6), position), (parts,), jnp.float32, low / len(pieces), top_value / len(pieces))
        return jnp.repeat(jnp.exp(draws), extent[position] // parts).reshape((-1,) + (1,) * (len(extent) - position - 1))

    loudness = one(*pieces[0])
    for cut in pieces[1:]:
        loudness = loudness * one(*cut)
    return loudness


def bell_draw(key, extent, deviation, bound, cuts=(), kind=jnp.bfloat16):
    gain = steps_of(key, extent, cuts, -0.22, 0.18) if cuts else 1.0
    values = jax.random.normal(key, extent, jnp.float32) * deviation * gain
    return jnp.minimum(jnp.maximum(values, -bound), bound).astype(kind)


def setup_inputs(seed: int = 0, part: int = 0) -> dict:
    seeds = jax.random.split(jax.random.key(seed), 6)
    part_keys = jax.random.split(jax.random.fold_in(seeds[5], part), 6)
    strain = bell_draw(part_keys[0], (2, DET, NH), 0.5, 4.0, ((2, 8),))
    templates = bell_draw(seeds[1], (2, KT, NH), 1.0, 6.0, ((1, 2), (2, 8)))
    lengths = plant(jax.random.randint(seeds[2], (KT,), NH // 4, NH + 1), jax.random.fold_in(seeds[2], 1), NH // 4, NH).astype(jnp.int32)
    antenna = jnp.clip(jax.random.uniform(seeds[3], (2, DET, SKY), jnp.float32, -1.0, 1.0) * steps_of(seeds[3], (2, DET, SKY), ((2, 2),), -0.4, 0.0), -1.0, 1.0).astype(jnp.bfloat16)
    delays = plant(jax.random.randint(seeds[4], (DET, SKY), -DM, DM + 1), jax.random.fold_in(seeds[4], 1), -DM, DM).astype(jnp.int32)
    return {"strain": strain, "templates": templates, "lengths": lengths, "antenna": antenna, "delays": delays}


TWO_PI = 6.283185307179586

def rounded(values):
    return lax.optimization_barrier(values.astype(jnp.bfloat16)).astype(jnp.float32)

def pick_row(series_row, index_rows):
    return series_row[index_rows]

def reference(strain, templates, lengths, antenna, delays):
    s_re = strain[0].astype(jnp.float32)
    s_im = strain[1].astype(jnp.float32)
    h_re = templates[0].astype(jnp.float32)
    h_im = templates[1].astype(jnp.float32)
    bin_ids = jnp.arange(NH, dtype=jnp.int32)
    in_band = (bin_ids[None, :] < lengths[:, None]).astype(jnp.float32)
    norm2 = lax.optimization_barrier(jnp.sum(in_band * (h_re * h_re + h_im * h_im), axis=1))
    x_re = rounded((h_re[:, None] * s_re[None] + h_im[:, None] * s_im[None]) * in_band[:, None])
    x_im = rounded((h_re[:, None] * s_im[None] - h_im[:, None] * s_re[None]) * in_band[:, None])
    spectrum = (x_re + 1j * x_im).reshape(KT, DET, N1 // 2, N2)
    sectioned = jnp.fft.ifft(spectrum, n=N1, axis=2) * N1
    t_first = jnp.arange(N1, dtype=jnp.int32)
    b_ids = jnp.arange(N2, dtype=jnp.int32)
    angle = (t_first[:, None] * b_ids[None, :]).astype(jnp.float32) * (TWO_PI / NF)
    cos_w = jnp.cos(angle)
    sin_w = jnp.sin(angle)
    y_re = rounded(sectioned.real * cos_w - sectioned.imag * sin_w)
    y_im = rounded(sectioned.real * sin_w + sectioned.imag * cos_w)
    t_second = jnp.arange(K2, dtype=jnp.int32)
    angle_two = (b_ids[:, None] * t_second[None, :]).astype(jnp.float32) * (TWO_PI / N2)
    cos_two = jnp.cos(angle_two)
    sin_two = jnp.sin(angle_two)
    highest = lax.Precision.HIGHEST
    z_re = jnp.einsum('kdab,bc->kdac', y_re, cos_two, precision=highest) - jnp.einsum('kdab,bc->kdac', y_im, sin_two, precision=highest)
    z_im = jnp.einsum('kdab,bc->kdac', y_re, sin_two, precision=highest) + jnp.einsum('kdab,bc->kdac', y_im, cos_two, precision=highest)
    scale = lax.rsqrt(norm2 + 1e-06)[:, None, None, None]
    zn_re = rounded(z_re * scale).transpose(0, 1, 3, 2).reshape(KT, DET, K2 * N1)
    zn_im = rounded(z_im * scale).transpose(0, 1, 3, 2).reshape(KT, DET, K2 * N1)
    sky_block = math.gcd(SKY, 256)
    block_count = SKY // sky_block
    weight_blocks = antenna.astype(jnp.float32).reshape(2, DET, block_count, sky_block).transpose(2, 0, 1, 3)
    delay_blocks = delays.reshape(DET, block_count, sky_block).transpose(1, 0, 2)
    times = N1 + jnp.arange(KO * N1, dtype=jnp.int32)

    def per_block(pair):
        weights, lags = pair
        where_ids = (times[None, None, :] + lags[:, :, None]).astype(jnp.int32)

        def per_template(best, series):
            series_re, series_im = series
            sel_re = jax.vmap(pick_row)(series_re, where_ids)
            sel_im = jax.vmap(pick_row)(series_im, where_ids)
            mix_re = jnp.einsum('pds,dst->pst', weights, sel_re, precision=highest)
            mix_im = jnp.einsum('pds,dst->pst', weights, sel_im, precision=highest)
            power = lax.optimization_barrier(jnp.sum(mix_re * mix_re + mix_im * mix_im, axis=0))
            return (jnp.maximum(best, power), None)
        start = jnp.zeros((sky_block, KO * N1), zn_re.dtype)
        best, unused = lax.scan(per_template, start, (zn_re, zn_im))
        return best
    result = lax.map(per_block, (weight_blocks, delay_blocks))
    return result.reshape(SKY, KO, N1).transpose(1, 2, 0)
```

```python
import functools

import jax
import jax.numpy as jnp
import numpy as np
from jax import lax
from jax.experimental import pallas as pl
from jax.experimental.pallas import tpu as pltpu
from jax.sharding import PartitionSpec as P

N1 = 2048
N2 = 512
DM = 48
NF = N1 * N2
LANE = 128
FINE = 16
TWO_PI = 2.0 * np.pi
CENTRE = N1 - DM + N1 // 2
MESH = pl.DeviceIdType.MESH
F32 = jnp.float32
BF16 = jnp.bfloat16


def host_table(rows, step, columns, period):
    phase = (np.arange(rows)[:, None] * step * columns[None, :]) % period
    angle = phase * (TWO_PI / period)
    return jnp.asarray(np.stack([np.cos(angle), np.sin(angle)]).astype(np.float32))


def outer_turn(coarse, fine):
    c_re, c_im = coarse[0], coarse[1]
    f_re, f_im = fine[0], fine[1]
    re, im = [], []
    for row in range(c_re.shape[0]):
        u, v = c_re[row : row + 1], c_im[row : row + 1]
        re.append(u * f_re - v * f_im)
        im.append(u * f_im + v * f_re)
    return jnp.concatenate(re, axis=0), jnp.concatenate(im, axis=0)


def transform_kernel(
    limits, s_ref, h_ref, pa_ref, pb_ref, bc_ref, bf_ref, ac_ref, af_ref, z_ref, x_ref, zs_ref, nrm_ref
):
    step = pl.program_id(0)
    blocks = pl.num_programs(0)
    temps, rows = h_ref.shape[1], h_ref.shape[2]
    dets = s_ref.shape[1]

    @pl.when(step == 0)
    def _():
        p_re, p_im = outer_full(pa_ref, pb_ref)
        ids = lax.broadcasted_iota(jnp.int32, (rows, N2), 0) * N2 + lax.broadcasted_iota(
            jnp.int32, (rows, N2), 1
        )
        for k in range(temps):
            keep = ids < limits[k]
            h_re = jnp.where(keep, h_ref[0, k].astype(F32), 0.0)
            h_im = jnp.where(keep, h_ref[1, k].astype(F32), 0.0)
            norm = jnp.sum(h_re * h_re + h_im * h_im, axis=0, keepdims=True)
            norm = jnp.broadcast_to(jnp.sum(norm, axis=1, keepdims=True), (1, LANE))
            high = norm.astype(BF16).astype(F32)
            nrm_ref[2 * k : 2 * k + 1] = high
            nrm_ref[2 * k + 1 : 2 * k + 2] = norm - high
            g_re = h_re * p_re + h_im * p_im
            g_im = h_re * p_im - h_im * p_re
            for d in range(dets):
                s_re = s_ref[0, d].astype(F32)
                s_im = s_ref[1, d].astype(F32)
                start = (k * dets + d) * 2 * rows
                x_ref[start : start + rows] = (g_re * s_re - g_im * s_im).astype(BF16)
                x_ref[start + rows : start + 2 * rows] = (g_re * s_im + g_im * s_re).astype(BF16)

    t_re, t_im = outer_turn(bc_ref[...], bf_ref[...])
    table = jnp.concatenate([t_re.astype(BF16), t_im.astype(BF16)], axis=1)
    a_re, a_im = outer_turn(ac_ref[...], af_ref[...])
    for item in range(temps * dets):
        start = item * 2 * rows
        r = jnp.dot(x_ref[start : start + 2 * rows], table, preferred_element_type=F32)
        c_re, s_re = r[:rows, :LANE], r[:rows, LANE:]
        c_im, s_im = r[rows:, :LANE], r[rows:, LANE:]
        u_re = jnp.sum(a_re * c_re - a_im * s_re, axis=0, keepdims=True)
        u_im = jnp.sum(a_re * c_im - a_im * s_im, axis=0, keepdims=True)
        v_re = jnp.sum(a_re * s_re + a_im * c_re, axis=0, keepdims=True)
        v_im = jnp.sum(a_re * s_im + a_im * c_im, axis=0, keepdims=True)
        zs_ref[0, 2 * item : 2 * item + 1] = u_re - v_im
        zs_ref[0, 2 * item + 1 : 2 * item + 2] = u_im + v_re
        zs_ref[1, 2 * item : 2 * item + 1] = u_re + v_im
        zs_ref[1, 2 * item + 1 : 2 * item + 2] = u_im - v_re
    tail = 2 * temps * dets
    zs_ref[0, tail : tail + 2 * temps] = nrm_ref[...]
    zs_ref[1, tail : tail + 2 * temps] = nrm_ref[...]
    flip = (
        lax.broadcasted_iota(jnp.int32, (LANE, LANE), 0)
        + lax.broadcasted_iota(jnp.int32, (LANE, LANE), 1)
        == LANE - 1
    )
    flip = jnp.where(flip, 1.0, 0.0).astype(BF16)
    ahead = jnp.dot(zs_ref[0].astype(BF16), flip, preferred_element_type=F32)
    z_ref[blocks - 1 - step] = ahead.astype(BF16)
    z_ref[blocks + step] = zs_ref[1].astype(BF16)


def outer_full(pa_ref, pb_ref):
    a_re, a_im = pa_ref[0], pa_ref[1]
    b_re, b_im = pb_ref[0], pb_ref[1]
    return a_re * b_re - a_im * b_im, a_re * b_im + a_im * b_re


def exchange_kernel(devices, skies, first, own, z_ref, got_ref, send_sem, recv_sem, local_sem):
    me = lax.axis_index("filt")
    side = lax.axis_index("sky")
    count = got_ref.shape[2]
    barrier = pltpu.get_barrier_semaphore()
    peers = [(o, q) for q in range(skies) for o in range(devices) if (o, q) != (0, 0)]
    for o, q in peers:
        pl.semaphore_signal(
            barrier,
            inc=1,
            device_id={"filt": lax.rem(me + o, devices), "sky": lax.rem(side + q, skies)},
            device_id_type=MESH,
        )
    pl.semaphore_wait(barrier, len(peers))

    def piece(target):
        return z_ref.at[pl.ds((first - own * target) // LANE, count)]

    mine = pltpu.make_async_copy(piece(me), got_ref.at[side, me], local_sem)
    mine.start()
    copies = []
    for n, (o, q) in enumerate(peers):
        target = lax.rem(me + o, devices)
        other = lax.rem(side + q, skies)
        copy = pltpu.make_async_remote_copy(
            src_ref=piece(target),
            dst_ref=got_ref.at[side, me],
            send_sem=send_sem.at[n],
            recv_sem=recv_sem.at[n],
            device_id={"filt": target, "sky": other},
            device_id_type=MESH,
        )
        copy.start()
        copies.append(copy)
    mine.wait()
    for n, (o, q) in enumerate(peers):
        source = lax.rem(me + devices - o, devices)
        other = lax.rem(side + skies - q, skies)
        pltpu.make_async_remote_copy(
            src_ref=piece(me),
            dst_ref=got_ref.at[other, source],
            send_sem=send_sem.at[n],
            recv_sem=recv_sem.at[n],
            device_id={"filt": source, "sky": other},
            device_id_type=MESH,
        ).wait_recv()
    for copy in copies:
        copy.wait_send()


def combine_kernel(dets, temps, first, shift_ref, got_ref, ant_ref, lag_ref, out_ref, a_ref):
    own, width = out_ref.shape[1], out_ref.shape[2]
    skies, devices, count = got_ref.shape[0], got_ref.shape[1], got_ref.shape[2]

    @pl.when(pl.program_id(0) == 0)
    def _():
        for g in range(skies):
            total = got_ref[g, 0].astype(F32)
            for j in range(1, devices):
                total = total + got_ref[g, j].astype(F32)
            line = jnp.concatenate([total[n] for n in range(count)], axis=1)
            if own % LANE or first % LANE:
                line = pltpu.roll(line, shift_ref[0], axis=1)
            tail = 2 * temps * dets
            for k in range(temps):
                norm = line[tail + 2 * k : tail + 2 * k + 1] + line[tail + 2 * k + 1 : tail + 2 * k + 2]
                scale = lax.rsqrt(norm + 1e-06)
                rows = line[2 * dets * k : 2 * dets * (k + 1)] * scale
                rows = rows.astype(BF16).astype(F32)
                for d in range(dets):
                    for c in range(2):
                        row = rows[2 * d + c : 2 * d + c + 1]
                        spread = jnp.broadcast_to(row, (own, count * LANE))
                        turned = pltpu.roll(spread, LANE, axis=1, stride=1, stride_axis=0)
                        a_ref[
                            g * temps + k, c * own : (c + 1) * own, d * LANE : (d + 1) * LANE
                        ] = turned[:, :LANE].astype(BF16)

    slot = lax.broadcasted_iota(jnp.int32, (LANE, width), 0)
    maps = [[], []]
    for d in range(dets):
        hit = slot == (LANE - 1 - DM) - lag_ref[d : d + 1]
        for p in range(2):
            weight = jnp.broadcast_to(ant_ref[p, d : d + 1].astype(F32), (LANE, width))
            maps[p].append(jnp.where(hit, weight, 0.0).astype(BF16))
    maps = [jnp.concatenate(m, axis=0) for m in maps]
    best = None
    for k in range(skies * temps):
        power = None
        for p in range(2):
            r = jnp.dot(a_ref[k], maps[p], preferred_element_type=F32)
            term = r[:own] * r[:own] + r[own:] * r[own:]
            power = term if power is None else power + term
        best = power if best is None else jnp.maximum(best, power)
    out_ref[0] = best


def body(strain, templates, lengths, antenna, delays):
    position = lax.axis_index("filt")
    devices = lax.axis_size("filt")
    skies = lax.axis_size("sky")
    temps = templates.shape[1]
    dets = strain.shape[1]
    bins = strain.shape[2]
    rows = bins // N2
    own = N1 // devices
    first_t = N1 - DM
    count = -(-own // LANE) + 1
    length = count * LANE
    reach = first_t + own * (devices - 1) + length - CENTRE
    half = -(-reach // LANE) * LANE
    blocks = half // LANE
    first = CENTRE + half - first_t - length
    ragged = own % LANE != 0
    got_count = count + 1 if ragged else count

    odd = 2 * np.arange(half) + 1
    b_coarse = host_table(N2 // FINE, FINE, odd, 2 * NF)
    b_fine = host_table(FINE, 1, odd, 2 * NF)
    a_fine = host_table(FINE, 1, odd, 2 * N1)
    turn = 2 * CENTRE - 1
    b_row = (np.arange(N2) * turn) % (2 * NF) * (TWO_PI / (2 * NF))
    pb = jnp.asarray(np.stack([np.cos(b_row), np.sin(b_row)])[:, None, :].astype(np.float32))
    a_ids = position * rows + lax.iota(jnp.int32, rows)
    a_angle = (a_ids * turn % (2 * N1)).astype(F32) * (TWO_PI / (2 * N1))
    pa = jnp.stack([jnp.cos(a_angle), jnp.sin(a_angle)])[:, :, None]
    c_ids = position * rows + FINE * lax.iota(jnp.int32, rows // FINE)
    c_phase = c_ids[:, None] * jnp.asarray(odd, jnp.int32)[None, :] % (2 * N1)
    c_angle = c_phase.astype(F32) * (TWO_PI / (2 * N1))
    a_coarse = jnp.stack([jnp.cos(c_angle), jnp.sin(c_angle)])

    limits = lengths - position * bins
    lines = 2 * temps * dets + 2 * temps

    def whole(shape):
        return pl.BlockSpec(shape, lambda g, *_: (0,) * len(shape))

    def columns(array):
        return pl.BlockSpec(array.shape[:2] + (LANE,), lambda g, *_: (0, 0, g))

    s4 = strain.reshape(2, dets, rows, N2)
    h4 = templates.reshape(2, temps, rows, N2)
    series = pl.pallas_call(
        transform_kernel,
        out_shape=jax.ShapeDtypeStruct((2 * blocks, lines, LANE), BF16),
        grid_spec=pltpu.PrefetchScalarGridSpec(
            num_scalar_prefetch=1,
            grid=(blocks,),
            in_specs=[
                whole(s4.shape),
                whole(h4.shape),
                whole(pa.shape),
                whole(pb.shape),
                columns(b_coarse),
                columns(b_fine),
                columns(a_coarse),
                columns(a_fine),
            ],
            out_specs=whole((2 * blocks, lines, LANE)),
            scratch_shapes=[
                pltpu.VMEM((temps * dets * 2 * rows, N2), BF16),
                pltpu.VMEM((2, lines, LANE), F32),
                pltpu.VMEM((2 * temps, LANE), F32),
            ],
        ),
        compiler_params=pltpu.CompilerParams(dimension_semantics=("arbitrary",)),
        name="transform",
    )(limits, s4, h4, pa, pb, b_coarse, b_fine, a_coarse, a_fine)
    if ragged:
        series = jnp.pad(series, ((0, 1), (0, 0), (0, 0)))

    peers = devices * skies - 1
    got = pl.pallas_call(
        functools.partial(exchange_kernel, devices, skies, first, own),
        out_shape=jax.ShapeDtypeStruct((skies, devices, got_count, lines, LANE), BF16),
        in_specs=[pl.BlockSpec(memory_space=pltpu.VMEM)],
        out_specs=pl.BlockSpec(memory_space=pltpu.VMEM),
        scratch_shapes=[
            pltpu.SemaphoreType.DMA((peers,)),
            pltpu.SemaphoreType.DMA((peers,)),
            pltpu.SemaphoreType.DMA,
        ],
        compiler_params=pltpu.CompilerParams(collective_id=0, has_side_effects=True),
        name="exchange",
    )(series)

    offset = (first - own * position) % LANE
    shift = jnp.reshape((got_count * LANE - offset) % (got_count * LANE), (1,)).astype(jnp.int32)
    if ragged:
        shift = (shift + LANE) % (got_count * LANE)
    sky_local = antenna.shape[2]
    width = 256 if sky_local % 256 == 0 else LANE
    return pl.pallas_call(
        functools.partial(combine_kernel, dets, temps, first),
        out_shape=jax.ShapeDtypeStruct((1, own, sky_local), F32),
        grid_spec=pltpu.PrefetchScalarGridSpec(
            num_scalar_prefetch=1,
            grid=(sky_local // width,),
            in_specs=[
                whole(got.shape),
                pl.BlockSpec((2, dets, width), lambda g, *_: (0, 0, g)),
                pl.BlockSpec((dets, width), lambda g, *_: (0, g)),
            ],
            out_specs=pl.BlockSpec((1, own, width), lambda g, *_: (0, 0, g)),
            scratch_shapes=[pltpu.VMEM((skies * temps, 2 * own, dets * LANE), BF16)],
        ),
        compiler_params=pltpu.CompilerParams(dimension_semantics=("arbitrary",)),
        name="combine",
    )(shift, got, antenna, delays)


def solution(mesh):
    in_specs = (
        P(None, "grp", "filt"),
        P(None, "sky", "filt"),
        P("sky"),
        P(None, None, "sky"),
        P(None, "sky"),
    )
    out_specs = P("grp", "filt", "sky")
    return jax.shard_map(body, mesh=mesh, in_specs=in_specs, out_specs=out_specs, check_vma=False)
```

```python
import functools

import jax
import jax.numpy as jnp
import numpy as np
from jax import lax
from jax.experimental import pallas as pl
from jax.experimental.pallas import tpu as pltpu
from jax.sharding import PartitionSpec as P

N1 = 2048
N2 = 512
DM = 48
NF = N1 * N2
LANE = 128
FINE = 16
TWO_PI = 2.0 * np.pi
CENTRE = N1 - DM + N1 // 2
MESH = pl.DeviceIdType.MESH
F32 = jnp.float32
BF16 = jnp.bfloat16


def host_table(rows, step, columns, period):
    phase = (np.arange(rows)[:, None] * step * columns[None, :]) % period
    angle = phase * (TWO_PI / period)
    return jnp.asarray(np.stack([np.cos(angle), np.sin(angle)]).astype(np.float32))


def outer_turn(coarse, fine):
    c_re, c_im = coarse[0], coarse[1]
    f_re, f_im = fine[0], fine[1]
    re, im = [], []
    for row in range(c_re.shape[0]):
        u, v = c_re[row : row + 1], c_im[row : row + 1]
        re.append(u * f_re - v * f_im)
        im.append(u * f_im + v * f_re)
    return jnp.concatenate(re, axis=0), jnp.concatenate(im, axis=0)


def transform_kernel(
    devices, skies, first, own, lengths, s_ref, h_ref, pa_ref, pb_ref, bc_ref, bf_ref, ac_ref, af_ref, rot_ref,
    out_ref, x_ref, zs_ref, nrm_ref, z_ref, got_ref, send_sem, recv_sem, local_sem,
):
    step = pl.program_id(0)
    blocks = z_ref.shape[0] // 2
    temps, rows = h_ref.shape[1], h_ref.shape[2]
    dets = s_ref.shape[0]
    count = got_ref.shape[2]
    me = lax.axis_index("filt")
    side = lax.axis_index("sky")
    barrier = pltpu.get_barrier_semaphore()
    peers = [(o, q) for q in range(skies) for o in range(devices) if (o, q) != (0, 0)]

    @pl.when(step == 0)
    def _():
        for o, q in peers:
            pl.semaphore_signal(
                barrier,
                inc=1,
                device_id={"filt": lax.rem(me + o, devices), "sky": lax.rem(side + q, skies)},
                device_id_type=MESH,
            )
        p_re, p_im = outer_full(pa_ref, pb_ref)
        ids = lax.broadcasted_iota(jnp.int32, (rows, N2), 0) * N2 + lax.broadcasted_iota(
            jnp.int32, (rows, N2), 1
        )
        for k in range(temps):
            keep = ids < lengths[k] - me * (rows * N2)
            h_re = jnp.where(keep, h_ref[0, k].astype(F32), 0.0)
            h_im = jnp.where(keep, h_ref[1, k].astype(F32), 0.0)
            norm = jnp.sum(h_re * h_re + h_im * h_im, axis=0, keepdims=True)
            norm = jnp.broadcast_to(jnp.sum(norm, axis=1, keepdims=True), (1, LANE))
            high = norm.astype(BF16).astype(F32)
            nrm_ref[2 * k : 2 * k + 1] = high
            nrm_ref[2 * k + 1 : 2 * k + 2] = norm - high
            g_re = h_re * p_re + h_im * p_im
            g_im = h_re * p_im - h_im * p_re
            for d in range(dets):
                s_re = s_ref[d, 0].astype(F32)
                s_im = s_ref[d, 1].astype(F32)
                start = (k * dets + d) * 2 * rows
                x_ref[start : start + rows] = (g_re * s_re - g_im * s_im).astype(BF16)
                x_ref[start + rows : start + 2 * rows] = (g_re * s_im + g_im * s_re).astype(BF16)

    def send(target, q):
        return pltpu.make_async_remote_copy(
            src_ref=z_ref.at[pl.ds((first - own * target) // LANE, count)],
            dst_ref=got_ref.at[side, me],
            send_sem=send_sem.at[target * skies + q],
            recv_sem=recv_sem.at[side * devices + me],
            device_id={"filt": target, "sky": lax.rem(side + q, skies)},
            device_id_type=MESH,
        )

    def keep_own():
        return pltpu.make_async_copy(
            z_ref.at[pl.ds((first - own * me) // LANE, count)], got_ref.at[side, me], local_sem
        )

    def ready(target):
        begin = (first - own * target) // LANE
        last = min(begin + count, 2 * blocks) - 1
        return max(blocks - 1 - begin, last - blocks)

    def send_all(when):
        for target in range(devices):
            if ready(target) == when:
                pl.when(target != me)(lambda target=target: send(target, 0).start())
                pl.when(target == me)(lambda: keep_own().start())
                for q in range(1, skies):
                    send(target, q).start()

    for when in range(blocks - 1):
        if any(ready(target) == when for target in range(devices)):
            @pl.when(step == when + 1)
            def _(when=when):
                if when == min(ready(target) for target in range(devices)):
                    pl.semaphore_wait(barrier, len(peers))
                send_all(when)

    t_re, t_im = outer_turn(bc_ref[...], bf_ref[...])
    table = jnp.concatenate([t_re.astype(BF16), t_im.astype(BF16)], axis=1)
    a_re, a_im = outer_turn(ac_ref[...], af_ref[...])
    up_re, up_im, dn_re, dn_im = [rot_ref[n, pl.ds(me, 1), :] for n in range(4)]
    for item in range(temps * dets):
        start = item * 2 * rows
        r = jnp.dot(x_ref[start : start + 2 * rows], table, preferred_element_type=F32)
        c_re, s_re = r[:rows, :LANE], r[:rows, LANE:]
        c_im, s_im = r[rows:, :LANE], r[rows:, LANE:]
        u_re = jnp.sum(a_re * c_re - a_im * s_re, axis=0, keepdims=True)
        u_im = jnp.sum(a_re * c_im - a_im * s_im, axis=0, keepdims=True)
        v_re = jnp.sum(a_re * s_re + a_im * c_re, axis=0, keepdims=True)
        v_im = jnp.sum(a_re * s_im + a_im * c_im, axis=0, keepdims=True)
        p_re, p_im = u_re - v_im, u_im + v_re
        m_re, m_im = u_re + v_im, u_im - v_re
        zs_ref[0, 2 * item : 2 * item + 1] = p_re * up_re - p_im * up_im
        zs_ref[0, 2 * item + 1 : 2 * item + 2] = p_re * up_im + p_im * up_re
        zs_ref[1, 2 * item : 2 * item + 1] = m_re * dn_re - m_im * dn_im
        zs_ref[1, 2 * item + 1 : 2 * item + 2] = m_re * dn_im + m_im * dn_re
    tail = 2 * temps * dets
    zs_ref[0, tail : tail + 2 * temps] = nrm_ref[...]
    zs_ref[1, tail : tail + 2 * temps] = nrm_ref[...]
    flip = (
        lax.broadcasted_iota(jnp.int32, (LANE, LANE), 0)
        + lax.broadcasted_iota(jnp.int32, (LANE, LANE), 1)
        == LANE - 1
    )
    flip = jnp.where(flip, 1.0, 0.0).astype(BF16)
    ahead = jnp.dot(zs_ref[0].astype(BF16), flip, preferred_element_type=F32)
    z_ref[blocks - 1 - step] = ahead.astype(BF16)
    z_ref[blocks + step] = zs_ref[1].astype(BF16)

    @pl.when(step == blocks - 1)
    def _():
        send_all(blocks - 1)
        keep_own().wait()
        for q in range(skies):
            for source in range(devices):
                def arrive(source=source, q=q):
                    other = lax.rem(side + q, skies)
                    pltpu.make_async_remote_copy(
                        src_ref=z_ref.at[pl.ds(0, count)],
                        dst_ref=got_ref.at[other, source],
                        send_sem=send_sem.at[source * skies + q],
                        recv_sem=recv_sem.at[other * devices + source],
                        device_id={"filt": source, "sky": other},
                        device_id_type=MESH,
                    ).wait_recv()
                if q:
                    arrive()
                else:
                    pl.when(source != me)(arrive)
        for g in range(skies):
            total = got_ref[g, 0].astype(F32)
            for j in range(1, devices):
                total = total + got_ref[g, j].astype(F32)
            out_ref[g] = total
        for target in range(devices):
            pl.when(target != me)(lambda target=target: send(target, 0).wait_send())
            for q in range(1, skies):
                send(target, q).wait_send()


def outer_full(pa_ref, pb_ref):
    rows = pa_ref.shape[1]
    a_re = jnp.concatenate([pa_ref[0]] * (N2 // LANE), axis=1)
    a_im = jnp.concatenate([pa_ref[1]] * (N2 // LANE), axis=1)
    b_re, b_im = pb_ref[0], pb_ref[1]
    return a_re * b_re - a_im * b_im, a_re * b_im + a_im * b_re


def combine_kernel(dets, temps, first, shift_ref, got_ref, ant_ref, lag_ref, out_ref, a_ref):
    own, width = out_ref.shape[1], out_ref.shape[2]
    skies, count = got_ref.shape[0], got_ref.shape[1]

    @pl.when(pl.program_id(0) == 0)
    def _():
        for g in range(skies):
            line = jnp.concatenate([got_ref[g, n] for n in range(count)], axis=1)
            if own % LANE or first % LANE:
                line = pltpu.roll(line, shift_ref[0], axis=1)
            tail = 2 * temps * dets
            for k in range(temps):
                norm = line[tail + 2 * k : tail + 2 * k + 1] + line[tail + 2 * k + 1 : tail + 2 * k + 2]
                scale = lax.rsqrt(norm + 1e-06)
                rows = line[2 * dets * k : 2 * dets * (k + 1)] * scale
                rows = rows.astype(BF16).astype(F32)
                for d in range(dets):
                    for c in range(2):
                        row = rows[2 * d + c : 2 * d + c + 1]
                        spread = jnp.broadcast_to(row, (own, count * LANE))
                        turned = pltpu.roll(spread, LANE, axis=1, stride=1, stride_axis=0)
                        a_ref[
                            g * temps + k, c * own : (c + 1) * own, d * LANE : (d + 1) * LANE
                        ] = turned[:, :LANE].astype(BF16)

    slot = lax.broadcasted_iota(jnp.int32, (LANE, width), 0)
    maps = [[], []]
    for d in range(dets):
        hit = slot == (LANE - 1 - DM) - lag_ref[d : d + 1]
        for p in range(2):
            weight = jnp.broadcast_to(ant_ref[d, p : p + 1].astype(F32), (LANE, width))
            maps[p].append(jnp.where(hit, weight, 0.0).astype(BF16))
    maps = [jnp.concatenate(m, axis=0) for m in maps]
    best = None
    for k in range(skies * temps):
        power = None
        for p in range(2):
            r = jnp.dot(a_ref[k], maps[p], preferred_element_type=F32)
            term = r[:own] * r[:own] + r[own:] * r[own:]
            power = term if power is None else power + term
        best = power if best is None else jnp.maximum(best, power)
    out_ref[0] = best


def body(strain, templates, lengths, antenna, delays):
    position = lax.axis_index("filt")
    devices = lax.axis_size("filt")
    skies = lax.axis_size("sky")
    temps = templates.shape[1]
    dets = strain.shape[1]
    bins = strain.shape[2]
    rows = bins // N2
    own = N1 // devices
    first_t = N1 - DM
    count = -(-own // LANE) + 1
    length = count * LANE
    reach = first_t + own * (devices - 1) + length - CENTRE
    half = -(-reach // LANE) * LANE
    blocks = half // LANE
    first = CENTRE + half - first_t - length
    ragged = own % LANE != 0
    got_count = count + 1 if ragged else count

    odd = 2 * np.arange(half) + 1
    b_coarse = host_table(N2 // FINE, FINE, odd, 2 * NF)
    b_fine = host_table(FINE, 1, odd, 2 * NF)
    a_fine = host_table(FINE, 1, odd, 2 * N1)
    turn = 2 * CENTRE - 1
    b_row = (np.arange(N2) * turn) % (2 * NF) * (TWO_PI / (2 * NF))
    pb = jnp.asarray(np.stack([np.cos(b_row), np.sin(b_row)])[:, None, :].astype(np.float32))
    pa = host_table(rows, turn, np.ones(LANE, np.int64), 2 * N1)
    a_coarse = host_table(rows // FINE, FINE, odd, 2 * N1)
    shifts = np.arange(devices)[:, None] * rows
    rot = []
    for sign in (1, -1):
        angle = shifts * (turn + sign * odd[None, :]) % (2 * N1) * (TWO_PI / (2 * N1))
        rot += [np.cos(angle), np.sin(angle)]
    rot = jnp.asarray(np.stack(rot).astype(np.float32))

    lines = 2 * temps * dets + 2 * temps

    def whole(shape):
        return pl.BlockSpec(shape, lambda g, *_: (0,) * len(shape))

    def columns(array):
        return pl.BlockSpec(array.shape[:2] + (LANE,), lambda g, *_: (0, 0, g))

    s4 = strain.transpose(1, 0, 2).reshape(dets, 2, rows, N2)
    h4 = templates.reshape(2, temps, rows, N2)
    peers = devices * skies
    got = pl.pallas_call(
        functools.partial(transform_kernel, devices, skies, first, own),
        out_shape=jax.ShapeDtypeStruct((skies, got_count, lines, LANE), F32),
        grid_spec=pltpu.PrefetchScalarGridSpec(
            num_scalar_prefetch=1,
            grid=(blocks,),
            in_specs=[
                whole(s4.shape),
                whole(h4.shape),
                whole(pa.shape),
                whole(pb.shape),
                columns(b_coarse),
                columns(b_fine),
                columns(a_coarse),
                columns(a_fine),
                columns(rot),
            ],
            out_specs=whole((skies, got_count, lines, LANE)),
            scratch_shapes=[
                pltpu.VMEM((temps * dets * 2 * rows, N2), BF16),
                pltpu.VMEM((2, lines, LANE), F32),
                pltpu.VMEM((2 * temps, LANE), F32),
                pltpu.VMEM((2 * blocks, lines, LANE), BF16),
                pltpu.VMEM((skies, devices, got_count, lines, LANE), BF16),
                pltpu.SemaphoreType.DMA((peers,)),
                pltpu.SemaphoreType.DMA((peers,)),
                pltpu.SemaphoreType.DMA,
            ],
        ),
        compiler_params=pltpu.CompilerParams(
            dimension_semantics=("arbitrary",), collective_id=0, has_side_effects=True
        ),
        name="transform",
    )(lengths, s4, h4, pa, pb, b_coarse, b_fine, a_coarse, a_fine, rot)

    offset = (first - own * position) % LANE
    shift = jnp.reshape((got_count * LANE - offset) % (got_count * LANE), (1,)).astype(jnp.int32)
    if ragged:
        shift = (shift + LANE) % (got_count * LANE)
    sky_local = antenna.shape[2]
    width = 256 if sky_local % 256 == 0 else LANE
    return pl.pallas_call(
        functools.partial(combine_kernel, dets, temps, first),
        out_shape=jax.ShapeDtypeStruct((1, own, sky_local), F32),
        grid_spec=pltpu.PrefetchScalarGridSpec(
            num_scalar_prefetch=1,
            grid=(sky_local // width,),
            in_specs=[
                whole(got.shape),
                pl.BlockSpec((dets, 2, width), lambda g, *_: (0, 0, g)),
                pl.BlockSpec((dets, width), lambda g, *_: (0, g)),
            ],
            out_specs=pl.BlockSpec((1, own, width), lambda g, *_: (0, 0, g)),
            scratch_shapes=[pltpu.VMEM((skies * temps, 2 * own, dets * LANE), BF16)],
        ),
        compiler_params=pltpu.CompilerParams(dimension_semantics=("arbitrary",)),
        name="combine",
    )(shift, got, antenna.transpose(1, 0, 2), delays)


def solution(mesh):
    in_specs = (
        P(None, "grp", "filt"),
        P(None, "sky", "filt"),
        P("sky"),
        P(None, None, "sky"),
        P(None, "sky"),
    )
    out_specs = P("grp", "filt", "sky")
    return jax.shard_map(body, mesh=mesh, in_specs=in_specs, out_specs=out_specs, check_vma=False)
```

```python
import functools

import jax
import jax.numpy as jnp
import numpy as np
from jax import lax
from jax.experimental import pallas as pl
from jax.experimental.pallas import tpu as pltpu
from jax.sharding import PartitionSpec as P

N1 = 2048
N2 = 512
DM = 48
NF = N1 * N2
LANE = 128
FINE = 16
TWO_PI = 2.0 * np.pi
CENTRE = N1 - DM + N1 // 2
MESH = pl.DeviceIdType.MESH
F32 = jnp.float32
BF16 = jnp.bfloat16


def host_table(rows, step, columns, period):
    phase = (np.arange(rows)[:, None] * step * columns[None, :]) % period
    angle = phase * (TWO_PI / period)
    return jnp.asarray(np.stack([np.cos(angle), np.sin(angle)]).astype(np.float32))


def transform_kernel(
    devices, skies, first, own, lengths, s_ref, h_ref, pa_ref, pb_ref, bc_ref, bf_ref, ac_ref, af_ref, rot_ref,
    out_ref, x_ref, t_ref, ph_ref, r_ref, zs_ref, nrm_ref, z_ref, got_ref, send_sem, recv_sem, local_sem,
):
    step = pl.program_id(0)
    blocks = z_ref.shape[0] // 2
    temps, rows = h_ref.shape[1], h_ref.shape[2]
    dets = s_ref.shape[0]
    count = got_ref.shape[2]
    me = lax.axis_index("filt")
    side = lax.axis_index("sky")
    barrier = pltpu.get_barrier_semaphore()
    peers = [(o, q) for q in range(skies) for o in range(devices) if (o, q) != (0, 0)]

    @pl.when(step == 0)
    def _():
        for o, q in peers:
            pl.semaphore_signal(
                barrier,
                inc=1,
                device_id={"filt": lax.rem(me + o, devices), "sky": lax.rem(side + q, skies)},
                device_id_type=MESH,
            )
        b_re, b_im = pb_ref[0], pb_ref[1]
        ids = lax.broadcasted_iota(jnp.int32, (FINE, N2), 0) * N2 + lax.broadcasted_iota(
            jnp.int32, (FINE, N2), 1
        )
        limits = [lengths[k] - me * (rows * N2) for k in range(temps)]

        def fill(chunk, norms):
            at = pl.ds(pl.multiple_of(chunk * FINE, FINE), FINE)
            a_re = jnp.concatenate([pa_ref[0, at, :]] * (N2 // LANE), axis=1)
            a_im = jnp.concatenate([pa_ref[1, at, :]] * (N2 // LANE), axis=1)
            p_re, p_im = a_re * b_re - a_im * b_im, a_re * b_im + a_im * b_re
            sums = []
            for k in range(temps):
                keep = ids < limits[k] - chunk * (FINE * N2)
                h_re = jnp.where(keep, h_ref[0, k, at, :].astype(F32), 0.0)
                h_im = jnp.where(keep, h_ref[1, k, at, :].astype(F32), 0.0)
                sums.append(norms[k] + (h_re * h_re + h_im * h_im))
                g_re = h_re * p_re + h_im * p_im
                g_im = h_re * p_im - h_im * p_re
                for d in range(dets):
                    s_re = s_ref[d, 0, at, :].astype(F32)
                    s_im = s_ref[d, 1, at, :].astype(F32)
                    start = (k * dets + d) * 2 * rows
                    up = pl.ds(pl.multiple_of(start + chunk * FINE, FINE), FINE)
                    low = pl.ds(pl.multiple_of(start + rows + chunk * FINE, FINE), FINE)
                    x_ref[up, :] = (g_re * s_re - g_im * s_im).astype(BF16)
                    x_ref[low, :] = (g_re * s_im + g_im * s_re).astype(BF16)
            return tuple(sums)

        norms = lax.fori_loop(
            0, rows // FINE, fill, tuple(jnp.zeros((FINE, N2), F32) for k in range(temps))
        )
        for k in range(temps):
            norm = jnp.sum(jnp.sum(norms[k], axis=0, keepdims=True), axis=1, keepdims=True)
            norm = jnp.broadcast_to(norm, (1, LANE))
            high = norm.astype(BF16).astype(F32)
            nrm_ref[2 * k : 2 * k + 1] = high
            nrm_ref[2 * k + 1 : 2 * k + 2] = norm - high

    def send(target, q):
        return pltpu.make_async_remote_copy(
            src_ref=z_ref.at[pl.ds((first - own * target) // LANE, count)],
            dst_ref=got_ref.at[side, me],
            send_sem=send_sem.at[target * skies + q],
            recv_sem=recv_sem.at[side * devices + me],
            device_id={"filt": target, "sky": lax.rem(side + q, skies)},
            device_id_type=MESH,
        )

    def keep_own():
        return pltpu.make_async_copy(
            z_ref.at[pl.ds((first - own * me) // LANE, count)], got_ref.at[side, me], local_sem
        )

    def ready(target):
        begin = (first - own * target) // LANE
        last = min(begin + count, 2 * blocks) - 1
        return max(blocks - 1 - begin, last - blocks)

    def send_all(when):
        for target in range(devices):
            if ready(target) == when:
                pl.when(target != me)(lambda target=target: send(target, 0).start())
                pl.when(target == me)(lambda: keep_own().start())
                for q in range(1, skies):
                    send(target, q).start()

    for when in range(blocks - 1):
        if any(ready(target) == when for target in range(devices)):
            @pl.when(step == when + 1)
            def _(when=when):
                if when == min(ready(target) for target in range(devices)):
                    pl.semaphore_wait(barrier, len(peers))
                send_all(when)

    def turned(coarse, fine, row):
        u, v = coarse[0, row : row + 1], coarse[1, row : row + 1]
        return u * fine[0] - v * fine[1], u * fine[1] + v * fine[0]

    b_fine = bf_ref[...]
    for row in range(N2 // FINE):
        t_re, t_im = turned(bc_ref, b_fine, row)
        t_ref[row * FINE : (row + 1) * FINE, :LANE] = t_re.astype(BF16)
        t_ref[row * FINE : (row + 1) * FINE, LANE:] = t_im.astype(BF16)
    a_fine = af_ref[...]
    for row in range(rows // FINE):
        a_re, a_im = turned(ac_ref, a_fine, row)
        ph_ref[0, row * FINE : (row + 1) * FINE] = a_re
        ph_ref[1, row * FINE : (row + 1) * FINE] = a_im
    r_ref[...] = jnp.dot(x_ref[...], t_ref[...], preferred_element_type=F32)
    up_re, up_im, dn_re, dn_im = [rot_ref[n, pl.ds(me, 1), :] for n in range(4)]
    for item in range(temps * dets):
        start = item * 2 * rows
        sums = [jnp.zeros((FINE, LANE), F32) for n in range(4)]
        for row in range(rows // FINE):
            at = slice(row * FINE, (row + 1) * FINE)
            up = slice(start + row * FINE, start + (row + 1) * FINE)
            low = slice(start + rows + row * FINE, start + rows + (row + 1) * FINE)
            a_re, a_im = ph_ref[0, at], ph_ref[1, at]
            c_re, s_re = r_ref[up, :LANE], r_ref[up, LANE:]
            c_im, s_im = r_ref[low, :LANE], r_ref[low, LANE:]
            sums[0] += a_re * c_re - a_im * s_re
            sums[1] += a_re * c_im - a_im * s_im
            sums[2] += a_re * s_re + a_im * c_re
            sums[3] += a_re * s_im + a_im * c_im
        u_re, u_im, v_re, v_im = [jnp.sum(n, axis=0, keepdims=True) for n in sums]
        p_re, p_im = u_re - v_im, u_im + v_re
        m_re, m_im = u_re + v_im, u_im - v_re
        zs_ref[0, 2 * item : 2 * item + 1] = p_re * up_re - p_im * up_im
        zs_ref[0, 2 * item + 1 : 2 * item + 2] = p_re * up_im + p_im * up_re
        zs_ref[1, 2 * item : 2 * item + 1] = m_re * dn_re - m_im * dn_im
        zs_ref[1, 2 * item + 1 : 2 * item + 2] = m_re * dn_im + m_im * dn_re
    tail = 2 * temps * dets
    zs_ref[0, tail : tail + 2 * temps] = nrm_ref[...]
    zs_ref[1, tail : tail + 2 * temps] = nrm_ref[...]
    flip = (
        lax.broadcasted_iota(jnp.int32, (LANE, LANE), 0)
        + lax.broadcasted_iota(jnp.int32, (LANE, LANE), 1)
        == LANE - 1
    )
    flip = jnp.where(flip, 1.0, 0.0).astype(BF16)
    ahead = jnp.dot(zs_ref[0].astype(BF16), flip, preferred_element_type=F32)
    z_ref[blocks - 1 - step] = ahead.astype(BF16)
    z_ref[blocks + step] = zs_ref[1].astype(BF16)

    @pl.when(step == blocks - 1)
    def _():
        send_all(blocks - 1)
        keep_own().wait()
        for q in range(skies):
            for source in range(devices):
                def arrive(source=source, q=q):
                    other = lax.rem(side + q, skies)
                    pltpu.make_async_remote_copy(
                        src_ref=z_ref.at[pl.ds(0, count)],
                        dst_ref=got_ref.at[other, source],
                        send_sem=send_sem.at[source * skies + q],
                        recv_sem=recv_sem.at[other * devices + source],
                        device_id={"filt": source, "sky": other},
                        device_id_type=MESH,
                    ).wait_recv()
                if q:
                    arrive()
                else:
                    pl.when(source != me)(arrive)
        for g in range(skies):
            total = got_ref[g, 0].astype(F32)
            for j in range(1, devices):
                total = total + got_ref[g, j].astype(F32)
            out_ref[g] = total
        for target in range(devices):
            pl.when(target != me)(lambda target=target: send(target, 0).wait_send())
            for q in range(1, skies):
                send(target, q).wait_send()


def combine_kernel(dets, temps, first, shift_ref, got_ref, ant_ref, lag_ref, out_ref, a_ref):
    own, width = out_ref.shape[1], out_ref.shape[2]
    skies, count = got_ref.shape[0], got_ref.shape[1]

    @pl.when(pl.program_id(0) == 0)
    def _():
        for g in range(skies):
            line = jnp.concatenate([got_ref[g, n] for n in range(count)], axis=1)
            if own % LANE or first % LANE:
                line = pltpu.roll(line, shift_ref[0], axis=1)
            tail = 2 * temps * dets
            for k in range(temps):
                norm = line[tail + 2 * k : tail + 2 * k + 1] + line[tail + 2 * k + 1 : tail + 2 * k + 2]
                scale = lax.rsqrt(norm + 1e-06)
                rows = line[2 * dets * k : 2 * dets * (k + 1)] * scale
                rows = rows.astype(BF16).astype(F32)
                for d in range(dets):
                    for c in range(2):
                        row = rows[2 * d + c : 2 * d + c + 1]
                        spread = jnp.broadcast_to(row, (own, count * LANE))
                        turned = pltpu.roll(spread, LANE, axis=1, stride=1, stride_axis=0)
                        a_ref[
                            g * temps + k, c * own : (c + 1) * own, d * LANE : (d + 1) * LANE
                        ] = turned[:, :LANE].astype(BF16)

    slot = lax.broadcasted_iota(jnp.int32, (LANE, width), 0)
    maps = [[], []]
    for d in range(dets):
        hit = slot == (LANE - 1 - DM) - lag_ref[d : d + 1]
        for p in range(2):
            weight = jnp.broadcast_to(ant_ref[d, p : p + 1].astype(F32), (LANE, width))
            maps[p].append(jnp.where(hit, weight, 0.0).astype(BF16))
    maps = [jnp.concatenate(m, axis=0) for m in maps]
    best = None
    for k in range(skies * temps):
        power = None
        for p in range(2):
            r = jnp.dot(a_ref[k], maps[p], preferred_element_type=F32)
            term = r[:own] * r[:own] + r[own:] * r[own:]
            power = term if power is None else power + term
        best = power if best is None else jnp.maximum(best, power)
    out_ref[0] = best


def body(strain, templates, lengths, antenna, delays):
    position = lax.axis_index("filt")
    devices = lax.axis_size("filt")
    skies = lax.axis_size("sky")
    temps = templates.shape[1]
    dets = strain.shape[1]
    bins = strain.shape[2]
    rows = bins // N2
    own = N1 // devices
    first_t = N1 - DM
    count = -(-own // LANE) + 1
    length = count * LANE
    reach = first_t + own * (devices - 1) + length - CENTRE
    half = -(-reach // LANE) * LANE
    blocks = half // LANE
    first = CENTRE + half - first_t - length
    ragged = own % LANE != 0
    got_count = count + 1 if ragged else count

    odd = 2 * np.arange(half) + 1
    b_coarse = host_table(N2 // FINE, FINE, odd, 2 * NF)
    b_fine = host_table(FINE, 1, odd, 2 * NF)
    a_fine = host_table(FINE, 1, odd, 2 * N1)
    turn = 2 * CENTRE - 1
    b_row = (np.arange(N2) * turn) % (2 * NF) * (TWO_PI / (2 * NF))
    pb = jnp.asarray(np.stack([np.cos(b_row), np.sin(b_row)])[:, None, :].astype(np.float32))
    pa = host_table(rows, turn, np.ones(LANE, np.int64), 2 * N1)
    a_coarse = host_table(rows // FINE, FINE, odd, 2 * N1)
    shifts = np.arange(devices)[:, None] * rows
    rot = []
    for sign in (1, -1):
        angle = shifts * (turn + sign * odd[None, :]) % (2 * N1) * (TWO_PI / (2 * N1))
        rot += [np.cos(angle), np.sin(angle)]
    rot = jnp.asarray(np.stack(rot).astype(np.float32))

    lines = 2 * temps * dets + 2 * temps

    def whole(shape):
        return pl.BlockSpec(shape, lambda g, *_: (0,) * len(shape))

    def columns(array):
        return pl.BlockSpec(array.shape[:2] + (LANE,), lambda g, *_: (0, 0, g))

    s4 = strain.transpose(1, 0, 2).reshape(dets, 2, rows, N2)
    h4 = templates.reshape(2, temps, rows, N2)
    peers = devices * skies
    got = pl.pallas_call(
        functools.partial(transform_kernel, devices, skies, first, own),
        out_shape=jax.ShapeDtypeStruct((skies, got_count, lines, LANE), F32),
        grid_spec=pltpu.PrefetchScalarGridSpec(
            num_scalar_prefetch=1,
            grid=(blocks,),
            in_specs=[
                whole(s4.shape),
                whole(h4.shape),
                whole(pa.shape),
                whole(pb.shape),
                columns(b_coarse),
                columns(b_fine),
                columns(a_coarse),
                columns(a_fine),
                columns(rot),
            ],
            out_specs=whole((skies, got_count, lines, LANE)),
            scratch_shapes=[
                pltpu.VMEM((temps * dets * 2 * rows, N2), BF16),
                pltpu.VMEM((N2, 2 * LANE), BF16),
                pltpu.VMEM((2, rows, LANE), F32),
                pltpu.VMEM((temps * dets * 2 * rows, 2 * LANE), F32),
                pltpu.VMEM((2, lines, LANE), F32),
                pltpu.VMEM((2 * temps, LANE), F32),
                pltpu.VMEM((2 * blocks, lines, LANE), BF16),
                pltpu.VMEM((skies, devices, got_count, lines, LANE), BF16),
                pltpu.SemaphoreType.DMA((peers,)),
                pltpu.SemaphoreType.DMA((peers,)),
                pltpu.SemaphoreType.DMA,
            ],
        ),
        compiler_params=pltpu.CompilerParams(
            dimension_semantics=("arbitrary",), collective_id=0, has_side_effects=True
        ),
        name="transform",
    )(lengths, s4, h4, pa, pb, b_coarse, b_fine, a_coarse, a_fine, rot)

    offset = (first - own * position) % LANE
    shift = jnp.reshape((got_count * LANE - offset) % (got_count * LANE), (1,)).astype(jnp.int32)
    if ragged:
        shift = (shift + LANE) % (got_count * LANE)
    sky_local = antenna.shape[2]
    width = 256 if sky_local % 256 == 0 else LANE
    return pl.pallas_call(
        functools.partial(combine_kernel, dets, temps, first),
        out_shape=jax.ShapeDtypeStruct((1, own, sky_local), F32),
        grid_spec=pltpu.PrefetchScalarGridSpec(
            num_scalar_prefetch=1,
            grid=(sky_local // width,),
            in_specs=[
                whole(got.shape),
                pl.BlockSpec((dets, 2, width), lambda g, *_: (0, 0, g)),
                pl.BlockSpec((dets, width), lambda g, *_: (0, g)),
            ],
            out_specs=pl.BlockSpec((1, own, width), lambda g, *_: (0, 0, g)),
            scratch_shapes=[pltpu.VMEM((skies * temps, 2 * own, dets * LANE), BF16)],
        ),
        compiler_params=pltpu.CompilerParams(dimension_semantics=("arbitrary",)),
        name="combine",
    )(shift, got, antenna.transpose(1, 0, 2), delays)


def solution(mesh):
    in_specs = (
        P(None, "grp", "filt"),
        P(None, "sky", "filt"),
        P("sky"),
        P(None, None, "sky"),
        P(None, "sky"),
    )
    out_specs = P("grp", "filt", "sky")
    return jax.shard_map(body, mesh=mesh, in_specs=in_specs, out_specs=out_specs, check_vma=False)
```
